256 devices in a mesh: ex: 32 (over z, y_lo, core), tok: 8 (over y_hi, x).
Axes of the slice: x: 4, y: 4 (y_hi: 2, y_lo: 2; y = y_hi * 2 + y_lo), z: 8, core: 2. Of those that a mesh axis runs over, the one named last changes fastest.
Arguments:
- activations: bfloat16 [8192, 32, 4096], P(('ex', 'tok')), may hold values from -6 to 6
- out_grads: bfloat16 [8192, 32, 2, 1024], P(('ex', 'tok')), may hold values from -6 to 6
- block_len: int32 [8192], P(('ex', 'tok')), may hold values from 1 to 32
- block_dest: int32 [8192, 1], P(('ex', 'tok')), may hold values from 0 to 31; in each aligned block of 32 rows (0 to 31, 32 to 63, ...) at most 2 rows name the same one
- block_slot: int32 [8192], P(('ex', 'tok')), may hold values from 0 to 3
- in_proj: bfloat16 [4096, 128], replicated, may hold values from -0.09375 to 0.09375
- out_proj: bfloat16 [2, 1024, 64], replicated, may hold values from -0.1875 to 0.1875
- query_grads: float32 [64, 8192], P('ex'), may hold values from -6 to 6
- precond: float32 [2, 2, 64, 64], replicated, may hold values from -2 to 2, as said below
Outputs:
- scores: float32 [64, 128], P('tok', 'ex')
The draws below stay inside these ranges and needn't reach their ends.
Inputs may be any that keep to these rules, and one draw needn't show every extreme that they name: `block_dest`: among the 32 blocks of one device no index of ex is named more than 2 times, a bound that some device reaches; every index of ex is named by some block of the whole array. `precond`: entries of order one or less.
All inputs are finite; a program needn't handle non-finite values.
Results may differ from the reference program's by a relative error of at most 0.0003.
Values sent between devices are 32-bit elements; how exact they have to be, the bound alone decides.
A program may use at most 64 MiB of HBM per device.

```python
import math
import jax
import jax.numpy as jnp
import numpy as np
from jax import lax

D = 4096
KV = 1024
R = 64
BLK = 32
NB = 32
CAP = 2
EX_DEV = 4
BLOCKS = 8192
EXAMPLES = 128
QRY = 64
F = 8192
N_EX = 32
N_TOK = 8


def draw_precond(key, part):
    first_key, second_key = jax.random.split(jax.random.fold_in(key, 17))
    diagonal = jax.random.uniform(first_key, (2, 2, R), jnp.float32, 0.6, 1.6)
    noise = jax.random.normal(second_key, (2, 2, R, R), jnp.float32)
    symmetric = (noise + jnp.swapaxes(noise, 2, 3)) * (0.35 / math.sqrt(2.0 * R))
    symmetric = jnp.clip(symmetric, -0.5, 0.5)
    identity = jnp.eye(R, dtype=jnp.float32)
    return symmetric * (1.0 - identity) + identity * diagonal[:, :, :, None]


def plant(result, key, smallest, largest):
    spot = [jax.random.randint(jax.random.fold_in(key, axis), (), 0, length) for axis, length in enumerate(result.shape)]
    longest = result.shape.index(max(result.shape))
    neighbour = spot[:longest] + [(spot[longest] + 1) % result.shape[longest]] + spot[longest + 1:]
    return result.at[tuple(spot)].set(smallest).at[tuple(neighbour)].set(largest)


def shard_levels(own_key, extent, cuts, least, top_value):
    loudness, own = 1.0, jax.random.fold_in(own_key, 6)
    for dim, blocks in cuts:
        draws = jnp.exp(jax.random.uniform(jax.random.fold_in(own, dim), (blocks,), jnp.float32, least / len(cuts), top_value / len(cuts)))
        loudness = loudness * jnp.repeat(draws, extent[dim] // blocks).reshape([-1 if axis == dim else 1 for axis in range(len(extent))])
    return loudness


def deal_out(own_key, own, number, rows, number_of, top, most, slope):
    order = jax.random.permutation(own_key, number_of)
    crowded, usual = shares(number_of, rows * top, most, slope, True), shares(number_of, rows * top, most, slope, False)
    places = jnp.arange(number_of)

    def named(tallies, turn):
        used = int((tallies > 0).sum())
        fixed = max(1, used // 4)
        shifted = fixed + (places - fixed + turn * (used - fixed)) % max(1, number_of - fixed)
        return jnp.zeros((number_of,), jnp.int32).at[order[jnp.where(places < fixed, places, shifted)]].set(jnp.asarray(tallies, jnp.int32))

    tallies = jnp.where(number % 4 == 0, named(crowded, number // 4), named(usual, number - number // 4 - 1))
    mixed = jax.random.permutation(jax.random.fold_in(own, 3), number_of)
    source_of, taker = mixed[0:number_of // 2 * 2:2], mixed[1:number_of // 2 * 2:2]
    room = jnp.minimum(tallies[source_of] - 1, most - tallies[taker]) // 2
    room = jnp.where((source_of == order[0]) | (taker == order[0]) | (tallies[taker] == 0), 0, jnp.maximum(room, 0))
    shifted = jax.random.randint(jax.random.fold_in(own, 4), (number_of // 2,), 0, 1 << 20) % (room + 1)
    tallies = tallies.at[source_of].add(-shifted).at[taker].add(shifted)
    labels = jnp.searchsorted(jnp.cumsum(tallies), jnp.arange(rows * top), side="right").astype(jnp.int32)
    listing = labels.reshape(top, rows).T
    listing = listing[jax.random.permutation(jax.random.fold_in(own, 1), rows)]
    turn = jax.random.randint(jax.random.fold_in(own, 2), (rows, 1), 0, top)
    return jnp.take_along_axis(listing, (jnp.arange(top)[None, :] + turn) % top, axis=1)


def shares(number_of, total, limit, slope, full):
    weights = [(1 << 20) // math.isqrt(rank ** slope) + 1 for rank in range(1, number_of + 1)]
    largest = limit if full else min(limit, max(-(-total // number_of), total * weights[0] // sum(weights)))
    least = 1 if total - largest >= number_of - 1 else 0
    counts, rest = [largest] + [least] * (number_of - 1), total - largest - least * (number_of - 1)
    while rest > 0:
        movable = [i for i in range(1, number_of) if counts[i] < largest] or [i for i in range(1, number_of) if counts[i] < limit]
        pool, left = sum([weights[i] for i in movable]), rest
        for i in movable:
            more = min(limit - counts[i], max(1, left * weights[i] // pool), rest)
            counts[i] = counts[i] + more
            rest = rest - more
    return np.array(counts)


def normal_values(rng, extent, width, limit, cuts=(), kind=jnp.bfloat16):
    values = width * jax.random.normal(rng, extent, jnp.float32)
    if cuts:
        values = values * shard_levels(rng, extent, cuts, -0.22, 0.18)
    return jnp.clip(values, -limit, limit).astype(kind)


def setup_inputs(seed: int = 0) -> dict:
    keys = jax.random.split(jax.random.key(seed), 10)
    activations = normal_values(keys[0], (BLOCKS, BLK, D), 1.0, 6.0, ((0, 256),))
    out_grads = normal_values(keys[1], (BLOCKS, BLK, 2, KV), 1.0, 6.0, ((0, 256),))
    block_len = plant(jax.random.randint(keys[2], (BLOCKS,), 1, BLK + 1), jax.random.fold_in(keys[2], 1), 1, BLK).astype(jnp.int32)
    block_dest_keys = jax.random.split(jax.random.fold_in(keys[3], 1), BLOCKS // NB)
    block_dest_turns = jax.random.permutation(jax.random.fold_in(keys[3], 3), BLOCKS // NB)
    block_dest = jax.vmap(lambda own, number: deal_out(jax.random.fold_in(keys[3], 2), own, number, NB, N_EX, 1, CAP, 2))(block_dest_keys, block_dest_turns).reshape((BLOCKS, 1))
    block_slot = plant(jax.random.randint(keys[4], (BLOCKS,), 0, EX_DEV), jax.random.fold_in(keys[4], 1), 0, EX_DEV - 1).astype(jnp.int32)
    in_proj = normal_values(keys[5], (D, 2 * R), D ** -0.5, 0.09375)
    out_proj = normal_values(keys[6], (2, KV, R), KV ** -0.5, 0.1875)
    query_grads = normal_values(keys[7], (QRY, F), 1.0, 6.0, ((0, 32),), jnp.float32)
    precond = draw_precond(jax.random.fold_in(keys[9], 71), 0)
    return dict(activations=activations, out_grads=out_grads, block_len=block_len, block_dest=block_dest, block_slot=block_slot, in_proj=in_proj, out_proj=out_proj, query_grads=query_grads, precond=precond)


highest = lax.Precision.HIGHEST


def block_terms(acts, grads, lens, in_proj, out_proj):
    count_blocks = acts.shape[0]
    size_block = acts.shape[1]
    proj_in = jnp.dot(acts.reshape(count_blocks * size_block, -1), in_proj, preferred_element_type=jnp.float32)
    proj_in = proj_in.reshape(count_blocks, size_block, 2, -1)
    proj_out = jnp.einsum("btlk,lkr->btlr", grads.astype(jnp.float32), out_proj.astype(jnp.float32), precision=highest)
    position = lax.broadcasted_iota(jnp.int32, (count_blocks, size_block), 1)
    live = (position < lens[:, None]).astype(jnp.float32)
    proj_out = proj_out * live[:, :, None, None]
    terms = jnp.einsum("btlo,btli->bloi", proj_out, proj_in, precision=highest)
    return terms.reshape(count_blocks, -1)


def reference(activations, out_grads, block_len, block_dest, block_slot, in_proj, out_proj, query_grads, precond):
    groups = N_EX * N_TOK

    def step(total, inputs):
        acts, grads, lens, target, owner_slot = inputs
        terms = block_terms(acts, grads, lens, in_proj, out_proj)
        example = target[:, 0] * EX_DEV + owner_slot
        onehot = (example[:, None] == jnp.arange(EXAMPLES, dtype=jnp.int32)[None, :]).astype(jnp.float32)
        return total + jnp.dot(onehot.T, terms, precision=highest), None

    features, _ = lax.scan(step, jnp.zeros((EXAMPLES, F), jnp.float32), (
        activations.reshape(groups, NB, BLK, D),
        out_grads.reshape(groups, NB, BLK, 2, KV),
        block_len.reshape(groups, NB),
        block_dest.reshape(groups, NB, 1),
        block_slot.reshape(groups, NB)))
    queries = query_grads.reshape(QRY, 2, R, R)
    left = jnp.einsum("lab,qlbc->qlac", precond[:, 0], queries, precision=highest)
    conditioned = jnp.einsum("qlac,lcd->qlad", left, precond[:, 1], precision=highest).reshape(QRY, F)
    return jnp.dot(conditioned, features.T, precision=highest) * (1.0 / (R * BLK))
```

```python
import jax
import jax.numpy as jnp
from jax import lax
from jax.experimental import pallas as pl
from jax.experimental.pallas import tpu as pltpu
from jax.sharding import PartitionSpec as P

f32 = jnp.float32
bf16 = jnp.bfloat16
NZ = 8
NB = 32
BLK = 32
ROWS = NB * BLK
D = 4096
KV = 1024
NCH = 8
CB = NB // NCH
CR = CB * BLK
MESH = pl.DeviceIdType.MESH


def split(x):
    hi = x.astype(bf16)
    return hi, (x - hi.astype(f32)).astype(bf16)


def dot(a, b, ca, cb, precision=None):
    return lax.dot_general(
        a, b, (((ca,), (cb,)), ((), ())), preferred_element_type=f32, precision=precision
    )


def body(
    act, grads, lens, dest, slot, win_h, wout_h, pre_h, q_h, out,
    abuf, gbuf, rbuf, G, qs, win, wout, pre, m0s, m1s, sbuf, r1, r2,
    csem, wsem, zsend, zrecv, ysend, yrecv, bsend, brecv, s1, v1, s2, v2,
):
    ex = lax.axis_index("ex")
    tok = lax.axis_index("tok")
    z, ylo, core = ex // 4, (ex // 2) % 2, ex % 2
    yhi, x = tok // 4, tok % 4
    y = yhi * 2 + ylo

    def block(zb, yl, c):
        return ((zb + 2 * NZ) % NZ * 2 + yl) * 2 + c

    def rows(eb, h):
        return qs.at[pl.ds(pl.multiple_of((eb * 2 + h) * 64, 64), 64)]

    def yneighbour(step):
        yn = (y + step + 4) % 4
        return (z * 4 + (yn % 2) * 2 + core, (yn // 2) * 4 + x)

    sibling = (z * 4 + ylo * 2 + (1 - core), tok)

    def zneighbour(step):
        return (((z + step + NZ) % NZ) * 4 + ylo * 2 + core, tok)

    plane = ((ylo * 2 + core) * 8) + tok

    def plane_peer(i):
        p = (plane + i) % 32
        return (z * 4 + p // 8, p % 8)

    def acopy(i):
        return pltpu.make_async_copy(act.at[pl.ds(i * CR, CR)], abuf.at[pl.ds(i * CR, CR)], csem.at[0, i])

    def gcopy(i):
        return pltpu.make_async_copy(grads.at[pl.ds(i * CR, CR)], gbuf.at[pl.ds(i * CR, CR)], csem.at[1, i])

    qcopies = [
        pltpu.make_async_copy(q_h.at[:, j, :], rows(ex, j), wsem.at[j]) for j in range(2)
    ]
    wcopies = [
        pltpu.make_async_copy(s, d, wsem.at[2 + n])
        for n, (s, d) in enumerate(((win_h, win), (wout_h, wout), (pre_h, pre)))
    ]
    for c in qcopies:
        c.start()
    for c in reversed(wcopies):
        c.start()
    for i in range(NCH):
        acopy(i).start()
        gcopy(i).start()

    barrier = pltpu.get_barrier_semaphore()
    for i in range(1, 32):
        pl.semaphore_signal(barrier, inc=1, device_id=plane_peer(i), device_id_type=MESH)
    for i in range(1, NZ):
        pl.semaphore_signal(barrier, inc=1, device_id=zneighbour(i), device_id_type=MESH)

    def remote(src, dst, ss, rs, dev):
        return pltpu.make_async_remote_copy(
            src_ref=src, dst_ref=dst, send_sem=ss, recv_sem=rs, device_id=dev, device_id_type=MESH
        )

    def zcopy(s, d, h):
        r = rows(block(z - (1 - 2 * d) * s, ylo, core), h)
        return remote(r, r, zsend, zrecv.at[s, d, h], zneighbour(1 - 2 * d))

    def zarrival(s, d, h):
        r = rows(block(z - (1 - 2 * d) * s, ylo, core), h)
        return remote(r, r, zsend, zrecv.at[s - 1, d, h], zneighbour(1 - 2 * d))

    def offset(n):
        s, d = (n + 1) // 2, (n + 1) % 2
        return -(1 - 2 * d) * s

    def ycopy(n, h):
        r = rows(block(z + offset(n), ylo, core), h)
        return remote(r, r, ysend, yrecv.at[n, h], yneighbour(1 - 2 * h))

    def yarrival(n, h):
        r = rows(block(z + offset(n), 1 - ylo, core), h)
        return remote(r, r, ysend, yrecv.at[n, h], yneighbour(1 - 2 * h))

    def bcopy(n, o, h):
        r = rows(block(z + offset(n), ylo if o == 0 else 1 - ylo, core), h)
        return remote(r, r, bsend, brecv, sibling)

    def own():
        for h in range(2):
            qcopies[h].wait()
        pl.semaphore_wait(barrier, 38)
        for h in range(2):
            zcopy(0, 0, h).start()
            zcopy(0, 1, h).start()
            ycopy(0, h).start()
            bcopy(0, 0, h).start()

    def ring(s):
        for h in range(2):
            for d in range(2):
                n = 2 * s - 1 + d
                zarrival(s, d, h).wait_recv()
                if s < 3 or h == d:
                    zcopy(s, d, h).start()
                ycopy(n, h).start()
                bcopy(n, 0, h).start()

    def ring_last():
        for d in range(2):
            zarrival(4, d, d).wait_recv()
            ycopy(7, d).start()
            bcopy(7, 0, d).start()

    def across(ns):
        for n in ns:
            for h in range(2):
                yarrival(n, h).wait_recv()
                bcopy(n, 1, h).start()

    def factors():
        lane = lax.broadcasted_iota(jnp.int32, (64, 64), 1)
        row = lax.broadcasted_iota(jnp.int32, (64, 64), 0)
        order = ((row // 2 + (row % 2) * 32) == lane).astype(bf16)
        same = (row == lane).astype(bf16)
        zero = jnp.zeros((64, 64), bf16)
        for l in range(2):
            hi, lo = split(pre[l, 0])
            hi, lo = (dot(v, order, 1, 0).astype(bf16) for v in (hi, lo))
            hi, lo = (jnp.concatenate([v, zero] if l == 0 else [zero, v], axis=1) for v in (hi, lo))
            for n, v in enumerate((hi, hi, lo)):
                m0s[pl.ds(n * 128 + l * 64, 64)] = v
            hi, lo = split(pre[l, 1])
            hi, lo = (dot(same, v, 1, 1).astype(bf16) for v in (hi, lo))
            hi, lo = (
                jnp.concatenate([v, v, zero, zero] if l == 0 else [zero, zero, v, v], axis=1)
                for v in (hi, lo)
            )
            for n, v in enumerate((hi, hi, lo)):
                m1s[pl.ds(n * 128 + l * 64, 64)] = v

    def chunk(i, carry):
        lanes = lax.broadcasted_iota(jnp.int32, (CR, 128), 1)
        lane32 = lax.broadcasted_iota(jnp.int32, (32, 128), 1)
        t32 = lax.broadcasted_iota(jnp.int32, (32, 128), 0)
        r0 = pl.multiple_of(i * CR, CR)
        acopy(i).wait()
        pi = dot(abuf[pl.ds(r0, CR)], win[...], 1, 0)
        gcopy(i).wait()
        rbuf[...] = dot(gbuf[pl.ds(r0, CR)].reshape(2 * CR, KV), wout[...], 1, 1)
        po = jnp.where(lanes < 64, rbuf[pl.ds(0, CR, stride=2)], rbuf[pl.ds(1, CR, stride=2)])
        po = jnp.concatenate(
            [jnp.where(t32 < lens[i * CB + b], po[b * 32 : (b + 1) * 32], 0.0) for b in range(CB)],
            axis=0,
        )
        hi, lo = split(po)
        oh, ol = split(dot(jnp.concatenate([hi, lo, hi], axis=1), m0s[...], 1, 0))
        hi, lo = split(pi)
        ih, il = split(dot(jnp.concatenate([hi, lo, hi], axis=1), m1s[...], 1, 0))
        for b in range(CB):
            s = slice(b * 32, (b + 1) * 32)
            H = dot(
                jnp.concatenate([oh[s], oh[s], ol[s]], axis=0),
                jnp.concatenate([ih[s], il[s], ih[s]], axis=0),
                0,
                0,
            )
            k0 = pl.multiple_of((i * CB + b) * 64, 64)
            G[pl.ds(k0, 32)] = jnp.where(lane32 < 64, H[0:32, 0:128], H[32:64, 0:128])
            G[pl.ds(k0 + 32, 32)] = jnp.where(lane32 < 64, H[64:96, 128:256], H[96:128, 128:256])
        return carry

    def chunks(a, b):
        lax.fori_loop(a, b, chunk, 0)

    wcopies[2].wait()
    factors()
    wcopies[1].wait()
    wcopies[0].wait()
    chunks(0, 1)
    own()
    chunks(1, 2)
    ring(1)
    chunks(2, 3)
    ring(2)
    across([0])
    chunks(3, 4)
    ring(3)
    across([1, 2])
    chunks(4, 6)
    ring_last()
    across([3, 4])
    chunks(6, 8)
    across([5, 6, 7])
    whole = qs.at[pl.ds(0, 32 * 64)]
    remote(whole, whole, bsend, brecv, sibling).wait_recv()

    def score(c, acc):
        gh, gl = split(G[pl.ds(c, 32, stride=64)])
        qh, ql = split(qs[pl.ds(c, 64, stride=64)])
        return acc + dot(jnp.concatenate([qh, ql], axis=0), jnp.concatenate([gh, gl], axis=0), 1, 1)

    acc = lax.fori_loop(0, 64, score, jnp.zeros((128, 64), f32), unroll=8)
    example = jnp.zeros((64, 128), jnp.int32)
    row = lax.broadcasted_iota(jnp.int32, (64, 128), 0) % 32
    lane = lax.broadcasted_iota(jnp.int32, (64, 128), 1)
    for b in range(NB):
        example = jnp.where(row == b, dest[b] * 4 + slot[b], example)
    onehot = (example == lane).astype(f32)
    table = dot(acc, onehot, 1, 0, lax.Precision.HIGHEST)
    sbuf[...] = ((table[0:64] + table[64:128]) * (1.0 / 2048.0)).reshape(8, 8, 128)

    for i in range(1, 32):
        ed, td = plane_peer(i)
        remote(sbuf.at[td], r1.at[plane], s1, v1, (ed, td)).start()
    r1[plane] = sbuf[tok]
    tiles = r1.at[pl.ds(0, 31)]
    remote(tiles, tiles, s1, v1, sibling).wait_recv()
    r2[z] = jnp.sum(r1[...], axis=0)
    for i in range(1, NZ):
        remote(r2.at[z], r2.at[z], s2, v2, zneighbour(i)).start()
    tiles2 = r2.at[pl.ds(0, 7)]
    remote(tiles2, tiles2, s2, v2, sibling).wait_recv()
    total = jnp.sum(r2[...], axis=0)
    pick = (
        lax.broadcasted_iota(jnp.int32, (4, 128), 1)
        == lax.broadcasted_iota(jnp.int32, (4, 128), 0) + ex * 4
    ).astype(f32)
    out[...] = dot(pick, total, 1, 1, lax.Precision.HIGHEST)

    zs = qs.at[pl.ds(0, 14 * 64)]
    remote(zs, zs, zsend, brecv, sibling).wait_send()
    ys = qs.at[pl.ds(0, 16 * 64)]
    remote(ys, ys, ysend, brecv, sibling).wait_send()
    remote(whole, whole, bsend, brecv, sibling).wait_send()
    remote(tiles, tiles, s1, v1, sibling).wait_send()
    remote(tiles2, tiles2, s2, v2, sibling).wait_send()


def on_device(activations, out_grads, block_len, block_dest, block_slot, in_proj, out_proj, query, precond):
    anyspace = pl.BlockSpec(memory_space=pl.ANY)
    smem = pl.BlockSpec(memory_space=pltpu.SMEM)
    vmem = pl.BlockSpec(memory_space=pltpu.VMEM)
    dma = pltpu.SemaphoreType.DMA
    out = pl.pallas_call(
        body,
        out_shape=jax.ShapeDtypeStruct((4, 8), f32),
        in_specs=[anyspace, anyspace, smem, smem, smem, anyspace, anyspace, anyspace, anyspace],
        out_specs=vmem,
        scratch_shapes=[
            pltpu.VMEM((ROWS, D), bf16),
            pltpu.VMEM((ROWS, 2, KV), bf16),
            pltpu.VMEM((2 * CR, 128), f32),
            pltpu.VMEM((NB * 64, 128), f32),
            pltpu.VMEM((64 * 64, 128), f32),
            pltpu.VMEM((D, 128), bf16),
            pltpu.VMEM((128, KV), bf16),
            pltpu.VMEM((2, 2, 64, 64), f32),
            pltpu.VMEM((384, 128), bf16),
            pltpu.VMEM((384, 256), bf16),
            pltpu.VMEM((8, 8, 128), f32),
            pltpu.VMEM((32, 8, 128), f32),
            pltpu.VMEM((NZ, 8, 128), f32),
            dma((2, NCH)),
            dma((5,)),
            dma,
            dma((4, 2, 2)),
            dma,
            dma((NZ, 2)),
            dma,
            dma,
            dma,
            dma,
            dma,
            dma,
        ],
        compiler_params=pltpu.CompilerParams(
            collective_id=0, has_side_effects=True, vmem_limit_bytes=56 << 20
        ),
    )(
        activations.reshape(ROWS, D),
        out_grads.reshape(ROWS, 2, KV),
        block_len,
        block_dest.reshape(NB),
        block_slot,
        in_proj,
        out_proj.transpose(0, 2, 1).reshape(128, KV),
        precond,
        query.reshape(2, 64, 128).transpose(1, 0, 2),
    )
    return out.T


def solution(mesh):
    both = ("ex", "tok")
    placed = (
        P(both, None, None),
        P(both, None, None, None),
        P(both),
        P(both, None),
        P(both),
        P(),
        P(),
        P("ex", None),
        P(),
    )
    return jax.shard_map(
        on_device, mesh=mesh, in_specs=placed, out_specs=P("tok", "ex"), check_vma=False
    )
```

```python
import jax
import jax.numpy as jnp
from jax import lax
from jax.experimental import pallas as pl
from jax.experimental.pallas import tpu as pltpu
from jax.sharding import PartitionSpec as P

f32 = jnp.float32
bf16 = jnp.bfloat16
NZ = 8
NB = 32
BLK = 32
ROWS = NB * BLK
D = 4096
KV = 1024
NCH = 4
CB = NB // NCH
CR = CB * BLK
MESH = pl.DeviceIdType.MESH


def split(x):
    hi = x.astype(bf16)
    return hi, (x - hi.astype(f32)).astype(bf16)


def dot(a, b, ca, cb, precision=None):
    return lax.dot_general(
        a, b, (((ca,), (cb,)), ((), ())), preferred_element_type=f32, precision=precision
    )


ORDER = (1, -1, 2, -2, 3, -3, 4)


def body(
    act, grads, lens, dest, slot, win_h, wout_h, pre_h, q_h, out,
    abuf, gbuf, rbuf, pbuf, G, qs, win, wout, pre, m0s, m1s, oh, sbuf, r1, r2,
    csem, wsem, zsend, zrecv, xsend, xrecv, gsend, grecv, hsend, hrecv, s1, v1, s2, v2,
):
    ex = lax.axis_index("ex")
    tok = lax.axis_index("tok")
    z, ylo, core = ex // 4, (ex // 2) % 2, ex % 2
    yhi, x = tok // 4, tok % 4
    y = yhi * 2 + ylo
    half = x % 2

    def device(dz, dy, dx):
        yn, xn = (y + dy + 4) % 4, (x + dx + 4) % 4
        return (((z + dz + NZ) % NZ) * 4 + (yn % 2) * 2 + core, (yn // 2) * 4 + xn)

    sibling = (z * 4 + ylo * 2 + (1 - core), tok)

    def rows(dz, yl, j, start=0, size=64):
        m = ((z + dz + NZ) % NZ) * 2 + yl
        return qs.at[pl.ds(pl.multiple_of((m * 2 + j) * 64 + start, 16), size)]

    plane = (ylo * 2 + core) * 8 + tok

    def plane_peer(i):
        p = (plane + i) % 32
        return (z * 4 + p // 8, p % 8)

    def acopy(i):
        return pltpu.make_async_copy(act.at[pl.ds(i * CR, CR)], abuf.at[pl.ds(i * CR, CR)], csem.at[0, i])

    def gcopy(i):
        return pltpu.make_async_copy(grads.at[pl.ds(i * CR, CR)], gbuf.at[pl.ds(i * CR, CR)], csem.at[1, i])

    def remote(src, dst, ss, rs, dev):
        return pltpu.make_async_remote_copy(
            src_ref=src, dst_ref=dst, send_sem=ss, recv_sem=rs, device_id=dev, device_id_type=MESH
        )

    qcopies = [pltpu.make_async_copy(q_h.at[:, j, :], rows(0, ylo, j), wsem.at[j]) for j in range(2)]
    wcopies = [
        pltpu.make_async_copy(s, d, wsem.at[2 + n])
        for n, (s, d) in enumerate(((win_h, win), (wout_h, wout), (pre_h, pre)))
    ]
    for c in qcopies:
        c.start()
    wcopies[2].start()
    wcopies[0].start()
    acopy(0).start()
    wcopies[1].start()
    gcopy(0).start()
    for i in range(1, NCH):
        acopy(i).start()
        gcopy(i).start()

    barrier = pltpu.get_barrier_semaphore()
    for i in range(1, 32):
        pl.semaphore_signal(barrier, inc=1, device_id=plane_peer(i), device_id_type=MESH)
    for i in range(1, NZ):
        pl.semaphore_signal(barrier, inc=1, device_id=device(i, 0, 0), device_id_type=MESH)

    def zcopy(d):
        r = rows(0, ylo, half)
        return remote(r, r, zsend, zrecv.at[d % NZ], device(d, 0, 0))

    def zarrival(d):
        r = rows(-d, ylo, half)
        return remote(r, r, zsend, zrecv.at[d % NZ], device(d, 0, 0))

    def spread(dz, j, start, size, dy, dx):
        r = rows(dz, ylo, j, start, size)
        remote(r, r, xsend, xrecv, device(0, dy, dx)).start()

    def own():
        for c in qcopies:
            c.wait()
        pl.semaphore_wait(barrier, 38)
        for d in ORDER:
            zcopy(d).start()
        for j in range(2):
            spread(0, j, 0, 32, 1, 0)
            spread(0, j, 32, 32, -1, 0)

    def forward(d):
        zarrival(d).wait_recv()
        spread(-d, half, 0, 16, 1, 1)
        spread(-d, half, 16, 16, -1, 1)
        spread(-d, half, 32, 16, 1, -1)
        spread(-d, half, 48, 16, -1, -1)
        spread(-d, half, 0, 32, 0, 1)
        spread(-d, half, 32, 32, 0, -1)
        spread(-d, half, 0, 32, 1, 0)
        spread(-d, half, 32, 32, -1, 0)

    def factors():
        lane = lax.broadcasted_iota(jnp.int32, (64, 64), 1)
        row = lax.broadcasted_iota(jnp.int32, (64, 64), 0)
        order = ((row // 2 + (row % 2) * 32) == lane).astype(bf16)
        same = (row == lane).astype(bf16)
        zero = jnp.zeros((64, 64), bf16)
        for l in range(2):
            hi, lo = split(pre[l, 0])
            hi, lo = (dot(v, order, 1, 0).astype(bf16) for v in (hi, lo))
            hi, lo = (jnp.concatenate([v, zero] if l == 0 else [zero, v], axis=1) for v in (hi, lo))
            for n, v in enumerate((hi, hi, lo)):
                m0s[pl.ds(n * 128 + l * 64, 64)] = v
            hi, lo = split(pre[l, 1])
            hi, lo = (dot(same, v, 1, 1).astype(bf16) for v in (hi, lo))
            hi, lo = (
                jnp.concatenate([v, v, zero, zero] if l == 0 else [zero, zero, v, v], axis=1)
                for v in (hi, lo)
            )
            for n, v in enumerate((hi, hi, lo)):
                m1s[pl.ds(n * 128 + l * 64, 64)] = v

    def examples():
        example = jnp.zeros((NB, 128), jnp.int32)
        row = lax.broadcasted_iota(jnp.int32, (NB, 128), 0)
        lane = lax.broadcasted_iota(jnp.int32, (NB, 128), 1)
        for b in range(NB):
            example = jnp.where(row == b, dest[b] * 4 + slot[b], example)
        oh[pl.ds(0, NB)] = (example == lane).astype(f32)

    def project(i):
        acopy(i).wait()
        pbuf[...] = dot(abuf[pl.ds(i * CR, CR)], win[...], 1, 0)

    def blocks(i):
        lanes = lax.broadcasted_iota(jnp.int32, (CR, 128), 1)
        lane32 = lax.broadcasted_iota(jnp.int32, (32, 128), 1)
        t32 = lax.broadcasted_iota(jnp.int32, (32, 128), 0)
        gcopy(i).wait()
        rbuf[...] = dot(gbuf[pl.ds(i * CR, CR)].reshape(2 * CR, KV), wout[...], 1, 1)
        po = jnp.where(lanes < 64, rbuf[pl.ds(0, CR, stride=2)], rbuf[pl.ds(1, CR, stride=2)])
        po = jnp.concatenate(
            [jnp.where(t32 < lens[i * CB + b], po[b * 32 : (b + 1) * 32], 0.0) for b in range(CB)],
            axis=0,
        )
        hi, lo = split(po)
        oh_, ol = split(dot(jnp.concatenate([hi, lo, hi], axis=1), m0s[...], 1, 0))
        hi, lo = split(pbuf[...])
        ih, il = split(dot(jnp.concatenate([hi, lo, hi], axis=1), m1s[...], 1, 0))
        for b in range(CB):
            s = slice(b * 32, (b + 1) * 32)
            H = dot(
                jnp.concatenate([oh_[s], oh_[s], ol[s]], axis=0),
                jnp.concatenate([ih[s], il[s], ih[s]], axis=0),
                0,
                0,
            )
            k0 = (i * CB + b) * 64
            G[pl.ds(k0, 32)] = jnp.where(lane32 < 64, H[0:32, 0:128], H[32:64, 0:128])
            G[pl.ds(k0 + 32, 32)] = jnp.where(lane32 < 64, H[64:96, 128:256], H[96:128, 128:256])
        size = CB * 64
        remote(G.at[pl.ds(i * size, size)], G.at[pl.ds(NB * 64 + i * size, size)], gsend, grecv, sibling).start()

    own()
    examples()
    remote(oh.at[pl.ds(0, NB)], oh.at[pl.ds(NB, NB)], hsend, hrecv, sibling).start()
    wcopies[2].wait()
    factors()
    wcopies[0].wait()
    project(0)
    wcopies[1].wait()
    blocks(0)
    forward(ORDER[0])
    forward(ORDER[1])
    project(1)
    forward(ORDER[2])
    forward(ORDER[3])
    blocks(1)
    forward(ORDER[4])
    forward(ORDER[5])
    project(2)
    forward(ORDER[6])
    blocks(2)
    project(3)
    blocks(3)
    remote(oh.at[pl.ds(0, NB)], oh.at[pl.ds(NB, NB)], hsend, hrecv, sibling).wait()
    half_g = G.at[pl.ds(0, NB * 64)]
    remote(half_g, half_g, gsend, grecv, sibling).wait_recv()
    spreads = qs.at[pl.ds(0, 1472)]
    remote(spreads, spreads, xsend, xrecv, sibling).wait_recv()

    def score(c, acc):
        gh, gl = split(G[pl.ds(c, 2 * NB, stride=64)])
        qh, ql = split(qs[pl.ds(c, 32, stride=64)])
        return acc + dot(jnp.concatenate([qh, ql], axis=0), jnp.concatenate([gh, gl], axis=0), 1, 1)

    acc = lax.fori_loop(0, 64, score, jnp.zeros((64, 128), f32), unroll=8)
    which = oh[...]
    table = dot(acc, jnp.concatenate([which, which], axis=0), 1, 0, lax.Precision.HIGHEST)
    sbuf[...] = ((table[0:32] + table[32:64]) * (1.0 / 2048.0)).reshape(8, 4, 128)

    for i in range(1, 32):
        ed, td = plane_peer(i)
        remote(sbuf.at[td], r1.at[plane], s1, v1, (ed, td)).start()
    r1[plane] = sbuf[tok]
    tiles = r1.at[pl.ds(0, 31)]
    remote(tiles, tiles, s1, v1, sibling).wait_recv()
    for c in range(2):
        part = jnp.sum(r1[c * 8 : c * 8 + 8], axis=0) + jnp.sum(r1[16 + c * 8 : 24 + c * 8], axis=0)
        r2[z, 2 * c : 2 * c + 2] = part[0:2]
        r2[z, 4 + 2 * c : 6 + 2 * c] = part[2:4]
    for i in range(1, NZ):
        remote(r2.at[z], r2.at[z], s2, v2, device(i, 0, 0)).start()
    tiles2 = r2.at[pl.ds(0, 7)]
    remote(tiles2, tiles2, s2, v2, sibling).wait_recv()
    total = jnp.sum(r2[...], axis=0)
    pick = (
        lax.broadcasted_iota(jnp.int32, (4, 128), 1)
        == lax.broadcasted_iota(jnp.int32, (4, 128), 0) + ex * 4
    ).astype(f32)
    out[...] = dot(pick, total, 1, 1, lax.Precision.HIGHEST)

    zs = qs.at[pl.ds(0, 7 * 64)]
    remote(zs, zs, zsend, xrecv, sibling).wait_send()
    remote(spreads, spreads, xsend, xrecv, sibling).wait_send()
    remote(half_g, half_g, gsend, grecv, sibling).wait_send()
    remote(tiles, tiles, s1, v1, sibling).wait_send()
    remote(tiles2, tiles2, s2, v2, sibling).wait_send()


def on_device(activations, out_grads, block_len, block_dest, block_slot, in_proj, out_proj, query, precond):
    anyspace = pl.BlockSpec(memory_space=pl.ANY)
    smem = pl.BlockSpec(memory_space=pltpu.SMEM)
    vmem = pl.BlockSpec(memory_space=pltpu.VMEM)
    dma = pltpu.SemaphoreType.DMA
    out = pl.pallas_call(
        body,
        out_shape=jax.ShapeDtypeStruct((4, 8), f32),
        in_specs=[anyspace, anyspace, smem, smem, smem, anyspace, anyspace, anyspace, anyspace],
        out_specs=vmem,
        scratch_shapes=[
            pltpu.VMEM((ROWS, D), bf16),
            pltpu.VMEM((ROWS, 2, KV), bf16),
            pltpu.VMEM((2 * CR, 128), f32),
            pltpu.VMEM((CR, 128), f32),
            pltpu.VMEM((2 * NB * 64, 128), f32),
            pltpu.VMEM((32 * 64, 128), f32),
            pltpu.VMEM((D, 128), bf16),
            pltpu.VMEM((128, KV), bf16),
            pltpu.VMEM((2, 2, 64, 64), f32),
            pltpu.VMEM((384, 128), bf16),
            pltpu.VMEM((384, 256), bf16),
            pltpu.VMEM((2 * NB, 128), f32),
            pltpu.VMEM((8, 4, 128), f32),
            pltpu.VMEM((32, 4, 128), f32),
            pltpu.VMEM((NZ, 8, 128), f32),
            dma((2, NCH)),
            dma((5,)),
            dma,
            dma((NZ,)),
            dma,
            dma,
            dma,
            dma,
            dma,
            dma,
            dma,
            dma,
            dma,
            dma,
        ],
        compiler_params=pltpu.CompilerParams(
            collective_id=0, has_side_effects=True, vmem_limit_bytes=56 << 20
        ),
    )(
        activations.reshape(ROWS, D),
        out_grads.reshape(ROWS, 2, KV),
        block_len,
        block_dest.reshape(NB),
        block_slot,
        in_proj,
        out_proj.transpose(0, 2, 1).reshape(128, KV),
        precond,
        query.reshape(2, 64, 128).transpose(1, 0, 2),
    )
    return out.T


def solution(mesh):
    both = ("ex", "tok")
    placed = (
        P(both, None, None),
        P(both, None, None, None),
        P(both),
        P(both, None),
        P(both),
        P(),
        P(),
        P("ex", None),
        P(),
    )
    return jax.shard_map(
        on_device, mesh=mesh, in_specs=placed, out_specs=P("tok", "ex"), check_vma=False
    )
```

```python
import jax
import jax.numpy as jnp
from jax import lax
from jax.experimental import pallas as pl
from jax.experimental.pallas import tpu as pltpu
from jax.sharding import PartitionSpec as P

f32 = jnp.float32
bf16 = jnp.bfloat16
NZ = 8
NB = 32
BLK = 32
ROWS = NB * BLK
D = 4096
KV = 1024
NCH = 4
CB = NB // NCH
CR = CB * BLK
MESH = pl.DeviceIdType.MESH


def split(x):
    hi = x.astype(bf16)
    return hi, (x - hi.astype(f32)).astype(bf16)


def terms(x):
    hi = x.astype(bf16)
    rest = x - hi.astype(f32)
    mid = rest.astype(bf16)
    return jnp.concatenate([hi, mid, (rest - mid.astype(f32)).astype(bf16)], axis=1)


def dot(a, b, ca, cb, precision=None):
    return lax.dot_general(
        a, b, (((ca,), (cb,)), ((), ())), preferred_element_type=f32, precision=precision
    )


ORDER = (1, -1, 2, -2, 3, -3, 4)
PEERS = sorted(
    [(dy, dx, dc) for dy in (-1, 0, 1, 2) for dx in (-1, 0, 1, 2) for dc in (0, 1)],
    key=lambda p: -abs(p[0]) - abs(p[1]) - 0.1 * p[2],
)[:31]


def body(
    act, grads, lens_h, dest_h, slot_h, win_h, wout_h, pre_h, q_h, out,
    lens, dest, slot, abuf, gbuf, rbuf, pbuf, G, qs, win, wout, pre, m0s, m1s, gs, oh, sbuf, r1, r2,
    csem, wsem, zsend, zrecv, xsend, xrecv, gsend, grecv, hsend, hrecv, s1, v1, s2, v2,
):
    ex = lax.axis_index("ex")
    tok = lax.axis_index("tok")
    z, ylo, core = ex // 4, (ex // 2) % 2, ex % 2
    yhi, x = tok // 4, tok % 4
    y = yhi * 2 + ylo
    half = x % 2

    def device(dz, dy, dx):
        yn, xn = (y + dy + 4) % 4, (x + dx + 4) % 4
        return (((z + dz + NZ) % NZ) * 4 + (yn % 2) * 2 + core, (yn // 2) * 4 + xn)

    sibling = (z * 4 + ylo * 2 + (1 - core), tok)

    def rows(dz, yl, j, start=0, size=64):
        m = ((z + dz + NZ) % NZ) * 2 + yl
        return qs.at[pl.ds(pl.multiple_of((m * 2 + j) * 64 + start, 16), size)]

    plane = (ylo * 2 + core) * 8 + tok

    def plane_peer(i):
        dy, dx, dc = PEERS[i]
        e, t = device(0, dy, dx)
        return ((e // 2) * 2 + (core + dc) % 2, t)

    def acopy(i):
        return pltpu.make_async_copy(act.at[pl.ds(i * CR, CR)], abuf.at[pl.ds(i * CR, CR)], csem.at[0, i])

    def gcopy(i):
        return pltpu.make_async_copy(grads.at[pl.ds(i * CR, CR)], gbuf.at[pl.ds(i * CR, CR)], csem.at[1, i])

    def remote(src, dst, ss, rs, dev):
        return pltpu.make_async_remote_copy(
            src_ref=src, dst_ref=dst, send_sem=ss, recv_sem=rs, device_id=dev, device_id_type=MESH
        )

    qcopies = [pltpu.make_async_copy(q_h.at[:, j, :], rows(0, ylo, j), wsem.at[j]) for j in range(2)]
    wcopies = [
        pltpu.make_async_copy(s, d, wsem.at[2 + n])
        for n, (s, d) in enumerate(
            ((win_h, win), (wout_h, wout), (pre_h, pre), (lens_h, lens), (dest_h, dest), (slot_h, slot))
        )
    ]
    barrier = pltpu.get_barrier_semaphore()
    for d in reversed(ORDER):
        pl.semaphore_signal(barrier, inc=1, device_id=device(d, 0, 0), device_id_type=MESH)
    for i in range(31):
        pl.semaphore_signal(barrier, inc=1, device_id=plane_peer(i), device_id_type=MESH)

    for c in qcopies:
        c.start()
    for n in (2, 4, 5, 3, 0):
        wcopies[n].start()
    acopy(0).start()
    wcopies[1].start()
    gcopy(0).start()
    for i in range(1, NCH):
        acopy(i).start()
        gcopy(i).start()

    def zcopy(d):
        return remote(q_h.at[:, half, :], rows(0, ylo, half), zsend, zrecv.at[d % NZ], device(d, 0, 0))

    def zarrival(d):
        r = rows(-d, ylo, half)
        return remote(r, r, zsend, zrecv.at[d % NZ], device(d, 0, 0))

    def spread(dz, j, start, size, dy, dx):
        r = rows(dz, ylo, j, start, size)
        remote(r, r, xsend, xrecv, device(0, dy, dx)).start()

    def own():
        pl.semaphore_wait(barrier, 38)
        for d in ORDER:
            zcopy(d).start()
        for j in range(2):
            for k in range(2):
                remote(
                    q_h.at[pl.ds(k * 32, 32), j, :], rows(0, ylo, j, k * 32, 32), xsend, xrecv,
                    device(0, 1 - 2 * k, 0),
                ).start()

    def forward(d):
        zarrival(d).wait_recv()
        spread(-d, half, 0, 16, 1, 1)
        spread(-d, half, 16, 16, -1, 1)
        spread(-d, half, 32, 16, 1, -1)
        spread(-d, half, 48, 16, -1, -1)
        spread(-d, half, 0, 32, 0, 1)
        spread(-d, half, 32, 32, 0, -1)
        spread(-d, half, 0, 32, 1, 0)
        spread(-d, half, 32, 32, -1, 0)

    def factors():
        lane = lax.broadcasted_iota(jnp.int32, (64, 64), 1)
        row = lax.broadcasted_iota(jnp.int32, (64, 64), 0)
        order = ((row // 2 + (row % 2) * 32) == lane).astype(bf16)
        same = (row == lane).astype(bf16)
        zero = jnp.zeros((64, 64), bf16)
        for l in range(2):
            hi, lo = split(pre[l, 0])
            hi, lo = (dot(v, order, 1, 0).astype(bf16) for v in (hi, lo))
            hi, lo = (jnp.concatenate([v, zero] if l == 0 else [zero, v], axis=1) for v in (hi, lo))
            for n, v in enumerate((hi, hi, lo)):
                m0s[pl.ds(n * 128 + l * 64, 64)] = v
            hi, lo = split(pre[l, 1])
            hi, lo = (dot(same, v, 1, 1).astype(bf16) for v in (hi, lo))
            hi, lo = (
                jnp.concatenate([v, v, zero, zero] if l == 0 else [zero, zero, v, v], axis=1)
                for v in (hi, lo)
            )
            for n, v in enumerate((hi, hi, lo)):
                m1s[pl.ds(n * 128 + l * 64, 64)] = v

    def examples():
        example = jnp.zeros((NB, 128), jnp.int32)
        row = lax.broadcasted_iota(jnp.int32, (NB, 128), 0)
        lane = lax.broadcasted_iota(jnp.int32, (NB, 128), 1)
        for b in range(NB):
            example = jnp.where(row == b, dest[b] * 4 + slot[b], example)
        oh[pl.ds(0, NB)] = (example == lane).astype(f32)

    def project(i):
        acopy(i).wait()
        pbuf[...] = dot(abuf[pl.ds(i * CR, CR)], win[...], 1, 0)

    def blocks(i):
        lanes = lax.broadcasted_iota(jnp.int32, (CR, 128), 1)
        lane32 = lax.broadcasted_iota(jnp.int32, (32, 128), 1)
        t32 = lax.broadcasted_iota(jnp.int32, (32, 128), 0)
        gcopy(i).wait()
        rbuf[...] = dot(gbuf[pl.ds(i * CR, CR)].reshape(2 * CR, KV), wout[...], 1, 1)
        po = jnp.where(lanes < 64, rbuf[pl.ds(0, CR, stride=2)], rbuf[pl.ds(1, CR, stride=2)])
        po = jnp.concatenate(
            [jnp.where(t32 < lens[i * CB + b], po[b * 32 : (b + 1) * 32], 0.0) for b in range(CB)],
            axis=0,
        )
        hi, lo = split(po)
        oh_, ol = split(dot(jnp.concatenate([hi, lo, hi], axis=1), m0s[...], 1, 0))
        hi, lo = split(pbuf[...])
        ih, il = split(dot(jnp.concatenate([hi, lo, hi], axis=1), m1s[...], 1, 0))
        for b in range(CB):
            s = slice(b * 32, (b + 1) * 32)
            H = dot(
                jnp.concatenate([oh_[s], oh_[s], ol[s]], axis=0),
                jnp.concatenate([ih[s], il[s], ih[s]], axis=0),
                0,
                0,
            )
            k0 = (i * CB + b) * 64
            G[pl.ds(k0, 32)] = jnp.where(lane32 < 64, H[0:32, 0:128], H[32:64, 0:128])
            G[pl.ds(k0 + 32, 32)] = jnp.where(lane32 < 64, H[64:96, 128:256], H[96:128, 128:256])
        size = CB * 64
        remote(G.at[pl.ds(i * size, size)], G.at[pl.ds(NB * 64 + i * size, size)], gsend, grecv, sibling).start()

    def prepare(part):
        def some(o, carry):
            for u in range(8):
                hi, lo = split(G[pl.ds(part * NB * 64 + o * 8 + u, NB, stride=64)])
                r0 = pl.multiple_of((o * 8 + u) * 128 + part * 64, 64)
                gs[pl.ds(r0, NB)] = hi
                gs[pl.ds(r0 + NB, NB)] = lo
            return carry

        return some

    half_g = G.at[pl.ds(0, NB * 64)]
    hcopy = remote(oh.at[pl.ds(0, NB)], oh.at[pl.ds(NB, NB)], hsend, hrecv, sibling)
    wcopies[2].wait()
    factors()
    own()
    wcopies[4].wait()
    wcopies[5].wait()
    examples()
    hcopy.start()
    wcopies[3].wait()
    wcopies[0].wait()
    project(0)
    wcopies[1].wait()
    blocks(0)
    project(1)
    blocks(1)
    forward(ORDER[0])
    forward(ORDER[1])
    project(2)
    blocks(2)
    forward(ORDER[2])
    forward(ORDER[3])
    project(3)
    blocks(3)
    forward(ORDER[4])
    forward(ORDER[5])
    lax.fori_loop(0, 8, prepare(0), 0)
    forward(ORDER[6])
    hcopy.wait()
    remote(half_g, half_g, gsend, grecv, sibling).wait_recv()
    lax.fori_loop(0, 8, prepare(1), 0)
    spreads = qs.at[pl.ds(0, 1472)]
    remote(spreads, spreads, xsend, xrecv, sibling).wait_recv()

    for c in qcopies:
        c.wait()
    left = []
    right = []
    for c in range(64):
        left.append(jnp.concatenate(split(qs[pl.ds(c, 32, stride=64)]), axis=0))
        right.append(gs[pl.ds(c * 128, 128)])
    acc = dot(jnp.concatenate(left, axis=1), jnp.concatenate(right, axis=1), 1, 1)
    which = oh[...].astype(bf16)
    which = jnp.concatenate([which[:NB]] * 2 + [which[NB:]] * 2, axis=0)
    table = dot(terms(acc), jnp.concatenate([which] * 3, axis=0), 1, 0)
    sbuf[...] = ((table[0:32] + table[32:64]) * (1.0 / 2048.0)).reshape(8, 4, 128)

    for i in range(31):
        ed, td = plane_peer(i)
        remote(sbuf.at[td], r1.at[plane], s1, v1, (ed, td)).start()
    r1[plane] = sbuf[tok]
    tiles = r1.at[pl.ds(0, 31)]
    remote(tiles, tiles, s1, v1, sibling).wait_recv()
    for c in range(2):
        part = jnp.sum(r1[c * 8 : c * 8 + 8], axis=0) + jnp.sum(r1[16 + c * 8 : 24 + c * 8], axis=0)
        r2[z, 2 * c : 2 * c + 2] = part[0:2]
        r2[z, 4 + 2 * c : 6 + 2 * c] = part[2:4]
    for d in reversed(ORDER):
        remote(r2.at[z], r2.at[z], s2, v2, device(d, 0, 0)).start()
    tiles2 = r2.at[pl.ds(0, 7)]
    remote(tiles2, tiles2, s2, v2, sibling).wait_recv()
    total = jnp.sum(r2[...], axis=0)
    pick = (
        lax.broadcasted_iota(jnp.int32, (4, 128), 1)
        == lax.broadcasted_iota(jnp.int32, (4, 128), 0) + ex * 4
    ).astype(bf16)
    out[...] = dot(jnp.concatenate([pick] * 3, axis=1), terms(total), 1, 1)

    zs = qs.at[pl.ds(0, 7 * 64)]
    remote(zs, zs, zsend, xrecv, sibling).wait_send()
    remote(spreads, spreads, xsend, xrecv, sibling).wait_send()
    remote(half_g, half_g, gsend, grecv, sibling).wait_send()
    remote(tiles, tiles, s1, v1, sibling).wait_send()
    remote(tiles2, tiles2, s2, v2, sibling).wait_send()


def on_device(activations, out_grads, block_len, block_dest, block_slot, in_proj, out_proj, query, precond):
    anyspace = pl.BlockSpec(memory_space=pl.ANY)
    vmem = pl.BlockSpec(memory_space=pltpu.VMEM)
    dma = pltpu.SemaphoreType.DMA
    out = pl.pallas_call(
        body,
        out_shape=jax.ShapeDtypeStruct((4, 8), f32),
        in_specs=[anyspace] * 9,
        out_specs=vmem,
        scratch_shapes=[
            pltpu.SMEM((NB,), jnp.int32),
            pltpu.SMEM((NB,), jnp.int32),
            pltpu.SMEM((NB,), jnp.int32),
            pltpu.VMEM((ROWS, D), bf16),
            pltpu.VMEM((ROWS, 2, KV), bf16),
            pltpu.VMEM((2 * CR, 128), f32),
            pltpu.VMEM((CR, 128), f32),
            pltpu.VMEM((2 * NB * 64, 128), f32),
            pltpu.VMEM((32 * 64, 128), f32),
            pltpu.VMEM((D, 128), bf16),
            pltpu.VMEM((128, KV), bf16),
            pltpu.VMEM((2, 2, 64, 64), f32),
            pltpu.VMEM((384, 128), bf16),
            pltpu.VMEM((384, 256), bf16),
            pltpu.VMEM((64 * 128, 128), bf16),
            pltpu.VMEM((2 * NB, 128), f32),
            pltpu.VMEM((8, 4, 128), f32),
            pltpu.VMEM((32, 4, 128), f32),
            pltpu.VMEM((NZ, 8, 128), f32),
            dma((2, NCH)),
            dma((8,)),
            dma,
            dma((NZ,)),
            dma,
            dma,
            dma,
            dma,
            dma,
            dma,
            dma,
            dma,
            dma,
            dma,
        ],
        compiler_params=pltpu.CompilerParams(
            collective_id=0, has_side_effects=True, vmem_limit_bytes=56 << 20
        ),
    )(
        activations.reshape(ROWS, D),
        out_grads.reshape(ROWS, 2, KV),
        block_len,
        block_dest.reshape(NB),
        block_slot,
        in_proj,
        out_proj.transpose(0, 2, 1).reshape(128, KV),
        precond,
        query.reshape(2, 64, 128).transpose(1, 0, 2),
    )
    return out.T


def solution(mesh):
    both = ("ex", "tok")
    placed = (
        P(both, None, None),
        P(both, None, None, None),
        P(both),
        P(both, None),
        P(both),
        P(),
        P(),
        P("ex", None),
        P(),
    )
    return jax.shard_map(
        on_device, mesh=mesh, in_specs=placed, out_specs=P("tok", "ex"), check_vma=False
    )
```

```python
import jax
import jax.numpy as jnp
from jax import lax
from jax.experimental import pallas as pl
from jax.experimental.pallas import tpu as pltpu
from jax.sharding import PartitionSpec as P

f32 = jnp.float32
bf16 = jnp.bfloat16
NZ = 8
NB = 32
BLK = 32
ROWS = NB * BLK
D = 4096
KV = 1024
NCH = 4
CB = NB // NCH
CR = CB * BLK
MESH = pl.DeviceIdType.MESH


def split(x):
    hi = x.astype(bf16)
    return hi, (x - hi.astype(f32)).astype(bf16)


def terms(x):
    hi = x.astype(bf16)
    rest = x - hi.astype(f32)
    mid = rest.astype(bf16)
    return jnp.concatenate([hi, mid, (rest - mid.astype(f32)).astype(bf16)], axis=1)


def dot(a, b, ca, cb, precision=None):
    return lax.dot_general(
        a, b, (((ca,), (cb,)), ((), ())), preferred_element_type=f32, precision=precision
    )


ORDER = (1, -1, 2, -2, 4, 3, -3)
PEERS = sorted(
    [(dy, dx, dc) for dy in (-1, 0, 1, 2) for dx in (-1, 0, 1, 2) for dc in (0, 1)],
    key=lambda p: -abs(p[0]) - abs(p[1]) - 0.1 * p[2],
)[:31]


def body(
    act, grads, lens_h, dest_h, slot_h, win_h, wout_h, pre_h, q_h, out,
    lens, dest, slot, abuf, gbuf, rbuf, pbuf, G, qs, win, wout, pre, m0s, m1s, gs, oh, sbuf, r1, r2,
    csem, wsem, zsend, zrecv, xsend, xrecv, gsend, grecv, hsend, hrecv, s1, v1, s2, v2,
):
    ex = lax.axis_index("ex")
    tok = lax.axis_index("tok")
    z, ylo, core = ex // 4, (ex // 2) % 2, ex % 2
    yhi, x = tok // 4, tok % 4
    y = yhi * 2 + ylo
    half = x % 2

    def device(dz, dy, dx):
        yn, xn = (y + dy + 4) % 4, (x + dx + 4) % 4
        return (((z + dz + NZ) % NZ) * 4 + (yn % 2) * 2 + core, (yn // 2) * 4 + xn)

    sibling = (z * 4 + ylo * 2 + (1 - core), tok)

    def rows(dz, yl, j, start=0, size=64):
        m = ((z + dz + NZ) % NZ) * 2 + yl
        return qs.at[pl.ds(pl.multiple_of((m * 2 + j) * 64 + start, 16), size)]

    plane = (ylo * 2 + core) * 8 + tok

    def plane_peer(i):
        dy, dx, dc = PEERS[i]
        e, t = device(0, dy, dx)
        return ((e // 2) * 2 + (core + dc) % 2, t)

    def acopy(i):
        return pltpu.make_async_copy(act.at[pl.ds(i * CR, CR)], abuf.at[pl.ds(i * CR, CR)], csem.at[0, i])

    def gcopy(i):
        return pltpu.make_async_copy(grads.at[pl.ds(i * CR, CR)], gbuf.at[pl.ds(i * CR, CR)], csem.at[1, i])

    def remote(src, dst, ss, rs, dev):
        return pltpu.make_async_remote_copy(
            src_ref=src, dst_ref=dst, send_sem=ss, recv_sem=rs, device_id=dev, device_id_type=MESH
        )

    qcopies = [pltpu.make_async_copy(q_h.at[:, j, :], rows(0, ylo, j), wsem.at[j]) for j in range(2)]
    wcopies = [
        pltpu.make_async_copy(s, d, wsem.at[2 + n])
        for n, (s, d) in enumerate(
            ((win_h, win), (wout_h, wout), (pre_h, pre), (lens_h, lens), (dest_h, dest), (slot_h, slot))
        )
    ]
    barrier = pltpu.get_barrier_semaphore()
    for d in reversed(ORDER):
        pl.semaphore_signal(barrier, inc=1, device_id=device(d, 0, 0), device_id_type=MESH)
    for i in range(31):
        pl.semaphore_signal(barrier, inc=1, device_id=plane_peer(i), device_id_type=MESH)

    for c in qcopies:
        c.start()
    for n in (2, 4, 5, 3, 0):
        wcopies[n].start()
    acopy(0).start()
    wcopies[1].start()
    gcopy(0).start()
    for i in range(1, NCH):
        acopy(i).start()
        gcopy(i).start()

    def zcopy(d):
        return remote(q_h.at[:, half, :], rows(0, ylo, half), zsend, zrecv.at[d % NZ], device(d, 0, 0))

    def zarrival(d):
        r = rows(-d, ylo, half)
        return remote(r, r, zsend, zrecv.at[d % NZ], device(d, 0, 0))

    def spread(dz, j, start, size, dy, dx):
        r = rows(dz, ylo, j, start, size)
        remote(r, r, xsend, xrecv, device(0, dy, dx)).start()

    def own():
        pl.semaphore_wait(barrier, 38)
        for d in ORDER:
            zcopy(d).start()
        for j in range(2):
            for k in range(2):
                remote(
                    q_h.at[pl.ds(k * 32, 32), j, :], rows(0, ylo, j, k * 32, 32), xsend, xrecv,
                    device(0, 1 - 2 * k, 0),
                ).start()

    def forward(d):
        zarrival(d).wait_recv()
        spread(-d, half, 0, 16, 1, 1)
        spread(-d, half, 16, 16, -1, 1)
        spread(-d, half, 32, 16, 1, -1)
        spread(-d, half, 48, 16, -1, -1)
        spread(-d, half, 0, 32, 0, 1)
        spread(-d, half, 32, 32, 0, -1)
        spread(-d, half, 0, 32, 1, 0)
        spread(-d, half, 32, 32, -1, 0)

    def factors():
        lane = lax.broadcasted_iota(jnp.int32, (64, 64), 1)
        row = lax.broadcasted_iota(jnp.int32, (64, 64), 0)
        order = ((row // 2 + (row % 2) * 32) == lane).astype(bf16)
        same = (row == lane).astype(bf16)
        zero = jnp.zeros((64, 64), bf16)
        for l in range(2):
            hi, lo = split(pre[l, 0])
            hi, lo = (dot(v, order, 1, 0).astype(bf16) for v in (hi, lo))
            hi, lo = (jnp.concatenate([v, zero] if l == 0 else [zero, v], axis=1) for v in (hi, lo))
            for n, v in enumerate((hi, hi, lo)):
                m0s[pl.ds(n * 128 + l * 64, 64)] = v
            hi, lo = split(pre[l, 1])
            hi, lo = (dot(same, v, 1, 1).astype(bf16) for v in (hi, lo))
            hi, lo = (
                jnp.concatenate([v, v, zero, zero] if l == 0 else [zero, zero, v, v], axis=1)
                for v in (hi, lo)
            )
            for n, v in enumerate((hi, hi, lo)):
                m1s[pl.ds(n * 128 + l * 64, 64)] = v

    def examples():
        example = jnp.zeros((NB, 128), jnp.int32)
        row = lax.broadcasted_iota(jnp.int32, (NB, 128), 0)
        lane = lax.broadcasted_iota(jnp.int32, (NB, 128), 1)
        for b in range(NB):
            example = jnp.where(row == b, dest[b] * 4 + slot[b], example)
        oh[pl.ds(0, NB)] = (example == lane).astype(f32)

    def project(i):
        acopy(i).wait()
        pbuf[...] = dot(abuf[pl.ds(i * CR, CR)], win[...], 1, 0)

    def blocks(i):
        lanes = lax.broadcasted_iota(jnp.int32, (CR, 128), 1)
        lane32 = lax.broadcasted_iota(jnp.int32, (32, 128), 1)
        t32 = lax.broadcasted_iota(jnp.int32, (32, 128), 0)
        gcopy(i).wait()
        rbuf[...] = dot(gbuf[pl.ds(i * CR, CR)].reshape(2 * CR, KV), wout[...], 1, 1)
        po = jnp.where(lanes < 64, rbuf[pl.ds(0, CR, stride=2)], rbuf[pl.ds(1, CR, stride=2)])
        po = jnp.concatenate(
            [jnp.where(t32 < lens[i * CB + b], po[b * 32 : (b + 1) * 32], 0.0) for b in range(CB)],
            axis=0,
        )
        hi, lo = split(po)
        oh_, ol = split(dot(jnp.concatenate([hi, lo, hi], axis=1), m0s[...], 1, 0))
        hi, lo = split(pbuf[...])
        ih, il = split(dot(jnp.concatenate([hi, lo, hi], axis=1), m1s[...], 1, 0))
        for b in range(CB):
            s = slice(b * 32, (b + 1) * 32)
            H = dot(
                jnp.concatenate([oh_[s], oh_[s], ol[s]], axis=0),
                jnp.concatenate([ih[s], il[s], ih[s]], axis=0),
                0,
                0,
            )
            k0 = (i * CB + b) * 64
            G[pl.ds(k0, 32)] = jnp.where(lane32 < 64, H[0:32, 0:128], H[32:64, 0:128])
            G[pl.ds(k0 + 32, 32)] = jnp.where(lane32 < 64, H[64:96, 128:256], H[96:128, 128:256])
        size = CB * 64
        remote(G.at[pl.ds(i * size, size)], G.at[pl.ds(NB * 64 + i * size, size)], gsend, grecv, sibling).start()

    def prepare(part):
        def some(o, carry):
            for u in range(8):
                hi, lo = split(G[pl.ds(part * NB * 64 + o * 8 + u, NB, stride=64)])
                r0 = pl.multiple_of((o * 8 + u) * 128 + part * 64, 64)
                gs[pl.ds(r0, NB)] = hi
                gs[pl.ds(r0 + NB, NB)] = lo
            return carry

        return some

    half_g = G.at[pl.ds(0, NB * 64)]
    hcopy = remote(oh.at[pl.ds(0, NB)], oh.at[pl.ds(NB, NB)], hsend, hrecv, sibling)
    wcopies[2].wait()
    factors()
    own()
    wcopies[4].wait()
    wcopies[5].wait()
    examples()
    hcopy.start()
    wcopies[3].wait()
    wcopies[0].wait()
    project(0)
    wcopies[1].wait()
    blocks(0)
    project(1)
    blocks(1)
    forward(ORDER[0])
    forward(ORDER[1])
    project(2)
    blocks(2)
    forward(ORDER[2])
    forward(ORDER[3])
    project(3)
    blocks(3)
    forward(ORDER[4])
    forward(ORDER[5])
    lax.fori_loop(0, 8, prepare(0), 0)
    forward(ORDER[6])
    hcopy.wait()
    remote(half_g, half_g, gsend, grecv, sibling).wait_recv()
    lax.fori_loop(0, 8, prepare(1), 0)
    spreads = qs.at[pl.ds(0, 1472)]
    remote(spreads, spreads, xsend, xrecv, sibling).wait_recv()

    for c in qcopies:
        c.wait()
    left = []
    right = []
    for c in range(64):
        left.append(jnp.concatenate(split(qs[pl.ds(c, 32, stride=64)]), axis=0))
        right.append(gs[pl.ds(c * 128, 128)])
    acc = dot(jnp.concatenate(left, axis=1), jnp.concatenate(right, axis=1), 1, 1)
    which = oh[...].astype(bf16)
    which = jnp.concatenate([which[:NB]] * 2 + [which[NB:]] * 2, axis=0)
    table = dot(terms(acc), jnp.concatenate([which] * 3, axis=0), 1, 0)
    sbuf[...] = ((table[0:32] + table[32:64]) * (1.0 / 2048.0)).reshape(8, 4, 128)

    for i in range(31):
        ed, td = plane_peer(i)
        remote(sbuf.at[td], r1.at[plane], s1, v1, (ed, td)).start()
    r1[plane] = sbuf[tok]
    tiles = r1.at[pl.ds(0, 31)]
    remote(tiles, tiles, s1, v1, sibling).wait_recv()
    for c in range(2):
        part = jnp.sum(r1[c * 8 : c * 8 + 8], axis=0) + jnp.sum(r1[16 + c * 8 : 24 + c * 8], axis=0)
        r2[z, 2 * c : 2 * c + 2] = part[0:2]
        r2[z, 4 + 2 * c : 6 + 2 * c] = part[2:4]
    for d in reversed(ORDER):
        remote(r2.at[z], r2.at[z], s2, v2, device(d, 0, 0)).start()
    tiles2 = r2.at[pl.ds(0, 7)]
    remote(tiles2, tiles2, s2, v2, sibling).wait_recv()
    total = jnp.sum(r2[...], axis=0)
    pick = (
        lax.broadcasted_iota(jnp.int32, (4, 128), 1)
        == lax.broadcasted_iota(jnp.int32, (4, 128), 0) + ex * 4
    ).astype(bf16)
    out[...] = dot(jnp.concatenate([pick] * 3, axis=1), terms(total), 1, 1)

    zs = qs.at[pl.ds(0, 7 * 64)]
    remote(zs, zs, zsend, xrecv, sibling).wait_send()
    remote(spreads, spreads, xsend, xrecv, sibling).wait_send()
    remote(half_g, half_g, gsend, grecv, sibling).wait_send()
    remote(tiles, tiles, s1, v1, sibling).wait_send()
    remote(tiles2, tiles2, s2, v2, sibling).wait_send()


def on_device(activations, out_grads, block_len, block_dest, block_slot, in_proj, out_proj, query, precond):
    anyspace = pl.BlockSpec(memory_space=pl.ANY)
    vmem = pl.BlockSpec(memory_space=pltpu.VMEM)
    dma = pltpu.SemaphoreType.DMA
    out = pl.pallas_call(
        body,
        out_shape=jax.ShapeDtypeStruct((4, 8), f32),
        in_specs=[anyspace] * 9,
        out_specs=vmem,
        scratch_shapes=[
            pltpu.SMEM((NB,), jnp.int32),
            pltpu.SMEM((NB,), jnp.int32),
            pltpu.SMEM((NB,), jnp.int32),
            pltpu.VMEM((ROWS, D), bf16),
            pltpu.VMEM((ROWS, 2, KV), bf16),
            pltpu.VMEM((2 * CR, 128), f32),
            pltpu.VMEM((CR, 128), f32),
            pltpu.VMEM((2 * NB * 64, 128), f32),
            pltpu.VMEM((32 * 64, 128), f32),
            pltpu.VMEM((D, 128), bf16),
            pltpu.VMEM((128, KV), bf16),
            pltpu.VMEM((2, 2, 64, 64), f32),
            pltpu.VMEM((384, 128), bf16),
            pltpu.VMEM((384, 256), bf16),
            pltpu.VMEM((64 * 128, 128), bf16),
            pltpu.VMEM((2 * NB, 128), f32),
            pltpu.VMEM((8, 4, 128), f32),
            pltpu.VMEM((32, 4, 128), f32),
            pltpu.VMEM((NZ, 8, 128), f32),
            dma((2, NCH)),
            dma((8,)),
            dma,
            dma((NZ,)),
            dma,
            dma,
            dma,
            dma,
            dma,
            dma,
            dma,
            dma,
            dma,
            dma,
        ],
        compiler_params=pltpu.CompilerParams(
            collective_id=0, has_side_effects=True, vmem_limit_bytes=56 << 20
        ),
    )(
        activations.reshape(ROWS, D),
        out_grads.reshape(ROWS, 2, KV),
        block_len,
        block_dest.reshape(NB),
        block_slot,
        in_proj,
        out_proj.transpose(0, 2, 1).reshape(128, KV),
        precond,
        query.reshape(2, 64, 128).transpose(1, 0, 2),
    )
    return out.T


def solution(mesh):
    both = ("ex", "tok")
    placed = (
        P(both, None, None),
        P(both, None, None, None),
        P(both),
        P(both, None),
        P(both),
        P(),
        P(),
        P("ex", None),
        P(),
    )
    return jax.shard_map(
        on_device, mesh=mesh, in_specs=placed, out_specs=P("tok", "ex"), check_vma=False
    )
```
